32 devices in a mesh: gx: 8 (over z, x), gy: 4 (over y, core).
Axes of the slice: x: 2, y: 2, z: 4, core: 2. Of those that a mesh axis runs over, the one named last changes fastest.
Arguments:
- populations: float32 [19, 64, 256, 256], P(None, 'gx', 'gy'), may hold values from 0 to 0.6
- rotation_init: float32 [3], replicated, may hold values from -0.75 to 0.75
- slot_cell: int32 [3, 8, 4, 2048], P(None, 'gx', 'gy'), may hold values from 0 to 255, as said below
- slot_count: int32 [8, 4], P('gx', 'gy'), may hold values from 128 to 2048, as said below
- marker_arm: float32 [3, 8, 4, 2048], P(None, 'gx', 'gy'), may hold values from -1.7 to 1.7
- marker_area: float32 [8, 4, 2048], P('gx', 'gy'), may hold values from 0.3 to 3
- marker_fraction: float32 [8, 4, 2048], P('gx', 'gy'), may hold values from 0 to 1
Outputs:
- populations_next: float32 [19, 64, 256, 256], P(None, 'gx', 'gy')
- rotation: float32 [3, 3], replicated
The draws below stay inside these ranges and needn't reach their ends.
Inputs may be any that keep to these rules, and one draw needn't show every extreme that they name: `slot_cell`: slot s of slab (a, b) names a cell whose first coordinate lies in [a * 8, (a + 1) * 8) and whose second lies in [b * 64, (b + 1) * 64); the third is any; slots at or past slot_count hold cells too but carry no marker. `slot_count`: some slab has all 2048 slots live in every draw.
All inputs are finite; a program needn't handle non-finite values.
Results may differ from the reference program's by a relative error of at most 0.0001.
Values sent between devices are 32-bit elements; how exact they have to be, the bound alone decides.
No kernel may reach another device: no remote copies, remote signals or barrier semaphores. Data moves between devices by JAX's collectives and lax.ppermute only.
A program may use at most 128 MiB of HBM per device.

```python
import math
import jax
import jax.numpy as jnp
from jax import lax

Q = 19
CX = 8
CY = 64
NZ = 256
SLOTS = 2048
ITERS = 3
SLABS_X = 8
SLABS_Y = 4
NX = 64
NY = 256


VELOCITY_TABLE = ((0, 0, 0), (1, 0, 0), (-1, 0, 0), (0, 1, 0), (0, -1, 0), (0, 0, 1), (0, 0, -1), (1, 1, 0), (-1, -1, 0), (1, -1, 0), (-1, 1, 0), (1, 0, 1), (-1, 0, -1), (1, 0, -1), (-1, 0, 1), (0, 1, 1), (0, -1, -1), (0, 1, -1), (0, -1, 1))


WEIGHT_TABLE = (1.0 / 3.0,) + (1.0 / 18.0,) * 6 + (1.0 / 36.0,) * 12


def marker_cells(key):
    extent = (SLABS_X, SLABS_Y, SLOTS)
    slab_extent = (SLABS_X, SLABS_Y, 1)
    subkeys = jax.random.split(jax.random.fold_in(key, 11), 5)
    span_y = min(CY, 16)
    span_z = min(NZ, max(1, SLOTS // (CX * span_y)))
    slab_x = lax.broadcasted_iota(jnp.int32, extent, 0)
    slab_y = lax.broadcasted_iota(jnp.int32, extent, 1)
    start_y = jax.random.randint(subkeys[0], slab_extent, 0, CY - span_y + 1)
    start_z = jax.random.randint(subkeys[1], slab_extent, 0, NZ - span_z + 1)
    coord_x = slab_x * CX + jax.random.randint(subkeys[2], extent, 0, CX)
    coord_y = slab_y * CY + start_y + jax.random.randint(subkeys[3], extent, 0, span_y)
    coord_z = start_z + jax.random.randint(subkeys[4], extent, 0, span_z)
    return jnp.stack([coord_x, coord_y, coord_z]).astype(jnp.int32)


def unit_vector(key):
    halves = jax.random.split(key, 2)
    height = jax.random.uniform(halves[0], (), jnp.float32, -1.0, 1.0)
    azimuth = jax.random.uniform(halves[1], (), jnp.float32, -math.pi, math.pi)
    radius = jnp.sqrt(jnp.maximum(1.0 - height * height, 0.0))
    return jnp.stack([radius * jnp.cos(azimuth), radius * jnp.sin(azimuth), height])


def draw_populations(key, part):
    extent = (NX, NY, NZ)
    lengths = (NX, NY, NZ)
    subkeys = jax.random.split(jax.random.fold_in(key, 53), 4)
    places = [(lax.broadcasted_iota(jnp.float32, extent, number) + 0.5 - 0.5 * lengths[number]) / (0.5 * lengths[number]) for number in range(3)]
    spin_axis = unit_vector(subkeys[0])
    swirling = [spin_axis[1] * places[2] - spin_axis[2] * places[1], spin_axis[2] * places[0] - spin_axis[0] * places[2], spin_axis[0] * places[1] - spin_axis[1] * places[0]]
    offset_flow = jnp.zeros((3,), jnp.float32)
    mean_flow = [0.15 * swirling[number] + offset_flow[number] for number in range(3)]
    density = jax.random.uniform(subkeys[2], extent, jnp.float32, 0.8, 1.2)
    speed_sq = mean_flow[0] * mean_flow[0] + mean_flow[1] * mean_flow[1] + mean_flow[2] * mean_flow[2]
    members = []
    for member in range(19):
        step_x, step_y, step_z = VELOCITY_TABLE[member]
        projected = step_x * mean_flow[0] + step_y * mean_flow[1] + step_z * mean_flow[2]
        noise_key = jax.random.fold_in(subkeys[3], member)
        jitter = jax.random.uniform(noise_key, extent, jnp.float32, -0.3, 0.3)
        members.append(WEIGHT_TABLE[member] * density * (1.0 + 3.0 * projected + 4.5 * projected * projected - 1.5 * speed_sq) * (1.0 + jitter))
    return jnp.stack(members).astype(jnp.float32)


def draw_slot_cell(key, part):
    return marker_cells(key)


def draw_marker_arm(key, part):
    positions = marker_cells(key).astype(jnp.float32)
    extents = jnp.asarray([NX, NY, NZ], jnp.float32)[:, None, None, None]
    centred = (positions + 0.5 - 0.5 * extents) / (0.5 * extents)
    subkey = jax.random.fold_in(key, 41)
    jitter = 0.1 * jnp.clip(jax.random.normal(subkey, positions.shape, jnp.float32), -3.0, 3.0)
    result = centred + jitter
    return result.astype(jnp.float32)


def draw_slot_count(key, part):
    extent = (SLABS_X, SLABS_Y)
    subkeys = jax.random.split(jax.random.fold_in(key, 23), 4)
    sparse_count = jax.random.randint(subkeys[0], extent, SLOTS // 16, SLOTS // 3 + 1)
    dense_count = SLOTS - jax.random.randint(subkeys[1], extent, 0, SLOTS // 4 + 1)
    surface = jax.random.randint(subkeys[2], extent, 0, 4) == 0
    counts = jnp.where(surface, dense_count, sparse_count)
    chosen = jax.random.randint(subkeys[3], (), 0, SLABS_X * SLABS_Y)
    position = lax.broadcasted_iota(jnp.int32, extent, 0) * SLABS_Y + lax.broadcasted_iota(jnp.int32, extent, 1)
    return jnp.where(position == chosen, SLOTS, counts).astype(jnp.int32)


def draw_marker_area(key, part):
    extent = (SLABS_X, SLABS_Y, SLOTS)
    position = (lax.broadcasted_iota(jnp.int32, extent, 0) * SLABS_Y + lax.broadcasted_iota(jnp.int32, extent, 1)).astype(jnp.float32)
    growth = 1.0 + 2.0 * position / max(1, SLABS_X * SLABS_Y - 1)
    subkey = jax.random.fold_in(key, 37)
    sample = jnp.exp(jax.random.uniform(subkey, extent, jnp.float32, math.log(0.3), 0.0))
    return (sample * growth).astype(jnp.float32)


def levels(own_key, shape, pieces, least, largest):
    def one(dim, parts):
        steps = jax.random.uniform(jax.random.fold_in(jax.random.fold_in(own_key, 6), dim), (parts,), jnp.float32, least / len(pieces), largest / len(pieces))
        return jnp.repeat(jnp.exp(steps), shape[dim] // parts).reshape((-1,) + (1,) * (len(shape) - dim - 1))

    gain = one(*pieces[0])
    for cut in pieces[1:]:
        gain = gain * one(*cut)
    return gain


def bell_draw(own_key, dims, deviation, limit, dtype=jnp.bfloat16):
    values = deviation * jax.random.normal(own_key, dims, jnp.float32)
    return jnp.clip(values, min=-limit, max=limit).astype(dtype)


def setup_inputs(seed: int = 0) -> dict:
    streams_of = jax.random.split(jax.random.key(seed), 8)
    populations = draw_populations(jax.random.fold_in(streams_of[7], 71), 0)
    rotation_init = bell_draw(streams_of[1], (3,), 0.25, 0.75, jnp.float32)
    slot_cell = draw_slot_cell(jax.random.fold_in(streams_of[7], 71), 0)
    slot_count = draw_slot_count(jax.random.fold_in(streams_of[7], 71), 0)
    marker_arm = draw_marker_arm(jax.random.fold_in(streams_of[7], 71), 0)
    marker_area = draw_marker_area(jax.random.fold_in(streams_of[7], 71), 0)
    marker_fraction = jnp.clip(1.0 * jax.random.uniform(streams_of[6], (SLABS_X, SLABS_Y, SLOTS), jnp.float32) ** levels(streams_of[6], (SLABS_X, SLABS_Y, SLOTS), ((0, 8), (1, 4)), -0.2, 0.2), 0.0, 1.0)
    return {"populations": populations, "rotation_init": rotation_init, "slot_cell": slot_cell, "slot_count": slot_count, "marker_arm": marker_arm, "marker_area": marker_area, "marker_fraction": marker_fraction}


VELOCITY_TABLE = ((0, 0, 0), (1, 0, 0), (-1, 0, 0), (0, 1, 0), (0, -1, 0), (0, 0, 1), (0, 0, -1),
                  (1, 1, 0), (-1, -1, 0), (1, -1, 0), (-1, 1, 0), (1, 0, 1), (-1, 0, -1),
                  (1, 0, -1), (-1, 0, 1), (0, 1, 1), (0, -1, -1), (0, 1, -1), (0, -1, 1))
WEIGHT_TABLE = (1.0 / 3.0,) + (1.0 / 18.0,) * 6 + (1.0 / 36.0,) * 12
RELAX_TIME = 0.8
SPREAD_GAIN = 0.25
SPIN_GAIN = 0.5


def cross(first, second):
    return jnp.stack([first[1] * second[2] - first[2] * second[1],
                      first[2] * second[0] - first[0] * second[2],
                      first[0] * second[1] - first[1] * second[0]])


def reference(populations, rotation_init, slot_cell, slot_count, marker_arm, marker_area, marker_fraction):
    density = jnp.sum(populations, axis=0)
    momentum = []
    for axis_number in range(3):
        total = jnp.zeros_like(density)
        for member in range(Q):
            direction = VELOCITY_TABLE[member][axis_number]
            if direction != 0:
                total = total + direction * populations[member]
        momentum.append(total)
    velocity = jnp.stack(momentum) / density
    coord_x = slot_cell[0].reshape(-1).astype(jnp.int32)
    coord_y = slot_cell[1].reshape(-1).astype(jnp.int32)
    coord_z = slot_cell[2].reshape(-1).astype(jnp.int32)
    cell_low = (coord_x * NY + coord_y) * NZ + coord_z
    cell_high = (coord_x * NY + coord_y) * NZ + (coord_z + 1) % NZ
    active = lax.broadcasted_iota(jnp.int32, (SLABS_X, SLABS_Y, SLOTS), 2) < slot_count[:, :, None]
    weight = jnp.where(active, marker_area, jnp.zeros_like(marker_area)).reshape(-1)
    fraction = marker_fraction.reshape(-1)
    lever = marker_arm.reshape(3, -1)
    inertia = jnp.sum(weight * jnp.sum(lever * lever, axis=0))
    velocity_field = velocity.reshape(3, -1)
    spin = rotation_init
    history = []
    for step_index in range(ITERS):
        sampled = (1.0 - fraction) * velocity_field[:, cell_low] + fraction * velocity_field[:, cell_high]
        target = cross(spin[:, None], lever)
        impulse = weight * (target - sampled)
        velocity_field = velocity_field.at[:, cell_low].add(SPREAD_GAIN * (1.0 - fraction) * impulse)
        velocity_field = velocity_field.at[:, cell_high].add(SPREAD_GAIN * fraction * impulse)
        torque = -jnp.sum(cross(lever, impulse), axis=1)
        spin = spin + SPIN_GAIN * torque / inertia
        history.append(spin)
    velocity = velocity_field.reshape(3, NX, NY, NZ)
    speed_sq = jnp.sum(velocity * velocity, axis=0)
    outputs = []
    for member in range(Q):
        shift_x, shift_y, shift_z = VELOCITY_TABLE[member]
        projected = shift_x * velocity[0] + shift_y * velocity[1] + shift_z * velocity[2]
        equilibrium = WEIGHT_TABLE[member] * density * (1.0 + 3.0 * projected + 4.5 * projected * projected - 1.5 * speed_sq)
        relaxed = populations[member] - (populations[member] - equilibrium) / RELAX_TIME
        outputs.append(jnp.roll(relaxed, (shift_x, shift_y, shift_z), axis=(0, 1, 2)))
    return jnp.stack(outputs), jnp.stack(history)
```

```python
import jax
import jax.numpy as jnp
from jax import lax
from jax.experimental import pallas as pl
from jax.experimental.pallas import tpu as pltpu
from jax.sharding import PartitionSpec as P

Q = 19

VELOCITY_TABLE = (
    (0, 0, 0),
    (1, 0, 0),
    (-1, 0, 0),
    (0, 1, 0),
    (0, -1, 0),
    (0, 0, 1),
    (0, 0, -1),
    (1, 1, 0),
    (-1, -1, 0),
    (1, -1, 0),
    (-1, 1, 0),
    (1, 0, 1),
    (-1, 0, -1),
    (1, 0, -1),
    (-1, 0, 1),
    (0, 1, 1),
    (0, -1, -1),
    (0, 1, -1),
    (0, -1, 1),
)
WEIGHT_TABLE = (1.0 / 3.0,) + (1.0 / 18.0,) * 6 + (1.0 / 36.0,) * 12
RELAX_TIME = 0.8
SPREAD_GAIN = 0.25
SPIN_GAIN = 0.5
PLUS_X = [m for m in range(Q) if VELOCITY_TABLE[m][0] == 1]
MINUS_X = [m for m in range(Q) if VELOCITY_TABLE[m][0] == -1]
PLUS_Y = [m for m in range(Q) if VELOCITY_TABLE[m][1] == 1]
MINUS_Y = [m for m in range(Q) if VELOCITY_TABLE[m][1] == -1]
CORNERS = [m for m in range(Q) if VELOCITY_TABLE[m][0] != 0 and VELOCITY_TABLE[m][1] != 0]
LEVER, WEIGHT, FRACTION = 0, 3, 4
CELL, NEXT, PLANE, LOW, HIGH = 0, 1, 2, 3, 4
EDGE = 8


def ring(axis, steps):
    count = lax.axis_size(axis)
    return [(source, (source + steps) % count) for source in range(count)]


def diagonal(step_x, step_y):
    count_x, count_y = lax.axis_size("gx"), lax.axis_size("gy")
    return [
        (a * count_y + b, ((a + step_x) % count_x) * count_y + (b + step_y) % count_y)
        for a in range(count_x)
        for b in range(count_y)
    ]


def global_sum(value):
    for axis in ("gy", "gx"):
        count = lax.axis_size(axis)
        if count & (count - 1) == 0:
            bit = 1
            while bit < count:
                value = value + lax.ppermute(value, axis, [(i, i ^ bit) for i in range(count)])
                bit *= 2
        else:
            value = lax.psum(value, axis)
    return value


def cross_rows(first, second):
    return [
        first[1] * second[2] - first[2] * second[1],
        first[2] * second[0] - first[0] * second[2],
        first[0] * second[1] - first[1] * second[0],
    ]


def halves(value):
    high = value.astype(jnp.bfloat16)
    return high, (value - high.astype(jnp.float32)).astype(jnp.bfloat16)


def one_hot(hit):
    return jnp.where(hit, 1.0, 0.0).astype(jnp.bfloat16)


def depth_chunk(depth, ints, floats):
    ids = lax.broadcasted_iota(jnp.int32, (depth, ints.shape[1]), 0)
    fraction = floats[FRACTION : FRACTION + 1]
    low = jnp.where(ids == ints[LOW : LOW + 1], 1.0 - fraction, 0.0)
    return low + jnp.where(ids == ints[HIGH : HIGH + 1], fraction, 0.0)


def front(
    spin, pops, cols, ints, floats, density_out, velocity_out, vector_out, sums_out, mask, turned, gathered
):
    step = pl.program_id(0)
    size_x, size_y, depth = density_out.shape
    slots = ints.shape[1]
    chunk = slots // size_x
    total = pops[0, 0]
    momentum = [None, None, None]
    for member in range(1, Q):
        value = pops[member, 0]
        total = total + value
        for axis in range(3):
            direction = VELOCITY_TABLE[member][axis]
            if direction == 0:
                continue
            if momentum[axis] is None:
                momentum[axis] = value if direction > 0 else -value
            elif direction > 0:
                momentum[axis] = momentum[axis] + value
            else:
                momentum[axis] = momentum[axis] - value
    density_out[step] = total
    inverse = 1.0 / total
    for axis in range(3):
        velocity_out[axis, step] = momentum[axis] * inverse

    start = pl.multiple_of(step * chunk, 128)
    mine = ints[:, pl.ds(start, chunk)]

    def mask_rows(index, carry):
        row = pl.multiple_of(index * 128, 128)
        low = cols[pl.ds(row, 128), 0:1]
        high = cols[pl.ds(row, 128), 1:2]
        mask[0, pl.ds(row, 128), pl.ds(start, chunk)] = one_hot(low == mine[CELL : CELL + 1])
        mask[1, pl.ds(row, 128), pl.ds(start, chunk)] = one_hot(high == mine[CELL : CELL + 1])
        mask[2, pl.ds(row, 128), pl.ds(start, chunk)] = one_hot(low == mine[NEXT : NEXT + 1])
        return carry

    lax.fori_loop(0, slots // 128, mask_rows, 0)

    def overlap(value):
        fraction = floats[FRACTION : FRACTION + 1, :]
        low = (1.0 - fraction) * value
        high = fraction * value
        low_a, low_b = [part.astype(jnp.float32) for part in halves(low)]
        high_a, high_b = [part.astype(jnp.float32) for part in halves(high)]
        both = jnp.concatenate([low_a, high_a, low_b, high_b], axis=0).astype(jnp.bfloat16)
        only_high = jnp.concatenate([high_a, high_b], axis=0).astype(jnp.bfloat16)
        only_low = jnp.concatenate([low_a, low_b], axis=0).astype(jnp.bfloat16)

        def body(index, carry):
            at = pl.multiple_of(index * chunk, 128)
            here = pl.ds(at, chunk)
            same = jnp.dot(both, mask[0, :, here], preferred_element_type=jnp.float32)
            up = jnp.dot(only_high, mask[1, :, here], preferred_element_type=jnp.float32)
            down = jnp.dot(only_low, mask[2, :, here], preferred_element_type=jnp.float32)
            at_low = same[0:8] + same[16:24] + up[0:8] + up[8:16]
            at_high = same[8:16] + same[24:32] + down[0:8] + down[8:16]
            part = floats[FRACTION : FRACTION + 1, here]
            gathered[:, here] = (1.0 - part) * at_low + part * at_high
            return carry

        lax.fori_loop(0, size_x, body, 0)
        return gathered[...]

    @pl.when(step == size_x - 1)
    def _():
        planes = size_x * size_y
        for axis in range(3):
            field = velocity_out[axis].reshape(planes, depth).T
            high, low = halves(field)
            turned[2 * axis * depth : (2 * axis + 1) * depth] = high
            turned[(2 * axis + 1) * depth : (2 * axis + 2) * depth] = low

        def sample(index, carry):
            here = pl.ds(pl.multiple_of(index * chunk, 128), chunk)
            ids = lax.broadcasted_iota(jnp.int32, (planes, chunk), 0)
            table = one_hot(ids == ints[PLANE : PLANE + 1, here])
            weights = depth_chunk(depth, ints[:, here], floats[:, here])
            for axis in range(3):
                rows = jnp.dot(
                    turned[2 * axis * depth : (2 * axis + 2) * depth],
                    table,
                    preferred_element_type=jnp.float32,
                )
                rows = rows[:depth] + rows[depth:]
                gathered[axis : axis + 1, here] = jnp.sum(rows * weights, axis=0, keepdims=True)
            return carry

        lax.fori_loop(0, size_x, sample, 0)
        lever = [floats[LEVER + axis : LEVER + axis + 1, :] for axis in range(3)]
        weight = floats[WEIGHT : WEIGHT + 1, :]
        target = cross_rows([spin[0], spin[1], spin[2]], lever)
        error = [target[axis] - gathered[axis : axis + 1, :] for axis in range(3)]
        blank = jnp.zeros_like(weight)
        stacked = jnp.concatenate(error + lever + [blank, blank], axis=0)
        second = stacked - SPREAD_GAIN * overlap(weight * stacked)
        third = second - SPREAD_GAIN * overlap(weight * second)
        second_rows = [second[axis : axis + 1] for axis in range(6)]
        third_rows = [third[axis : axis + 1] for axis in range(3)]
        arm = [weight * row for row in lever]
        products = []
        for rows in (error, second_rows[:3], third_rows):
            products += cross_rows(arm, rows)
        for rows in (lever, second_rows[3:]):
            products += [rows[i] * arm[j] for i in range(3) for j in range(3)]
        products += [blank] * (32 - len(products))
        products = jnp.concatenate(products, axis=0)
        reduced = jnp.sum(products, axis=1, keepdims=True)
        row_ids = lax.broadcasted_iota(jnp.int32, (32, 128), 0)
        lane_ids = lax.broadcasted_iota(jnp.int32, (32, 128), 1)
        picked = jnp.where(row_ids == lane_ids, reduced, 0.0)
        sums_out[...] = jnp.sum(picked, axis=0, keepdims=True)
        static = [weight * (error[i] + second_rows[i] + third_rows[i]) for i in range(3)]
        moved = [weight * row for row in second_rows[3:]]
        vector_out[...] = jnp.concatenate(static + arm + moved + [blank] * 7, axis=0)


def back(spin, sums, ints, floats, vectors, density, velocity, *refs):
    members = refs[:Q]
    out, history, face_up, face_down, block_up, block_down, edge_up, edge_down = refs[Q : Q + 8]
    corner_out = refs[Q + 8 : Q + 12]
    field = refs[Q + 12]
    step = pl.program_id(0)
    size_x, size_y, depth = density.shape
    planes = size_x * size_y
    slots = ints.shape[1]
    chunk = slots // size_x

    @pl.when(step == 0)
    def _():
        entry = [sums[0:1, i : i + 1] for i in range(27)]
        direct, moved = entry[9:18], entry[18:27]
        inertia = direct[0] + direct[4] + direct[8]
        trace = moved[0] + moved[4] + moved[8]

        def turn(table, diagonal_sum, delta):
            return [
                diagonal_sum * delta[i]
                - (table[3 * i] * delta[0] + table[3 * i + 1] * delta[1] + table[3 * i + 2] * delta[2])
                for i in range(3)
            ]

        scale = -SPIN_GAIN / inertia
        first = [scale * value for value in entry[0:3]]
        extra = turn(direct, inertia, first)
        second = [scale * (entry[3 + i] + extra[i]) for i in range(3)]
        late = turn(moved, trace, first)
        extra = turn(direct, inertia, second)
        third = [scale * (entry[6 + i] + late[i] + extra[i]) for i in range(3)]
        row_ids = lax.broadcasted_iota(jnp.int32, (3, 3), 0)
        lane_ids = lax.broadcasted_iota(jnp.int32, (3, 3), 1)
        result = jnp.zeros((3, 3), jnp.float32)
        for axis in range(3):
            one = spin[axis] + first[axis]
            two = one + second[axis]
            three = two + third[axis]
            value = jnp.where(row_ids == 0, one, jnp.where(row_ids == 1, two, three))
            result = jnp.where(lane_ids == axis, value, result)
        history[...] = result
        both = [first[i] + second[i] for i in range(3)]
        for axis in range(3):
            field[axis] = velocity[axis].reshape(planes, depth)

        def spread(index, carry):
            here = pl.ds(pl.multiple_of(index * chunk, 128), chunk)
            lever = [vectors[3 + i : 4 + i, here] for i in range(3)]
            bent = [vectors[6 + i : 7 + i, here] for i in range(3)]
            plain = cross_rows(both, lever)
            after = cross_rows(first, bent)
            ids = lax.broadcasted_iota(jnp.int32, (planes, chunk), 0)
            table = one_hot(ids == ints[PLANE : PLANE + 1, here])
            weights = depth_chunk(depth, ints[:, here], floats[:, here])
            for axis in range(3):
                impulse = SPREAD_GAIN * (vectors[axis : axis + 1, here] + plain[axis] + after[axis])
                high, low = halves(weights * impulse)
                added = lax.dot_general(
                    table, high, (((1,), (1,)), ((), ())), preferred_element_type=jnp.float32
                )
                added = added + lax.dot_general(
                    table, low, (((1,), (1,)), ((), ())), preferred_element_type=jnp.float32
                )
                field[axis] = field[axis] + added
            return carry

        lax.fori_loop(0, size_x, spread, 0)

    def fields_at(place):
        place_rows = pl.ds(pl.multiple_of(place * size_y, 8), size_y)
        u = [field[axis, place_rows, :] for axis in range(3)]
        base = 1.0 - 1.5 * (u[0] * u[0] + u[1] * u[1] + u[2] * u[2])
        return u, base, density[place] * (1.0 / RELAX_TIME)

    for step_x in (0, 1, -1):
        place = lax.rem(step + (size_x - step_x), size_x)
        u, base, scaled = fields_at(place)
        for member in range(Q):
            velocity_here = VELOCITY_TABLE[member]
            if velocity_here[0] != step_x:
                continue
            projected = None
            for axis in range(3):
                if velocity_here[axis] == 0:
                    continue
                term = u[axis] if velocity_here[axis] > 0 else -u[axis]
                projected = term if projected is None else projected + term
            shape = base
            if projected is not None:
                shape = base + projected * (3.0 + 4.5 * projected)
            value = (1.0 - 1.0 / RELAX_TIME) * members[member][0, 0] + (
                WEIGHT_TABLE[member] * scaled
            ) * shape
            if velocity_here[1] != 0:
                value = pltpu.roll(value, velocity_here[1] % size_y, 0)
            if velocity_here[2] != 0:
                value = pltpu.roll(value, velocity_here[2] % depth, 1)
            out[member, 0] = value
            if velocity_here[1] == 1:
                number = PLUS_Y.index(member)
                block_up[number, pl.ds(step, 1)] = value[None, :EDGE]
                edge_up[number, pl.ds(step, 1)] = value[None, 0:1]
            if velocity_here[1] == -1:
                number = MINUS_Y.index(member)
                block_down[number, pl.ds(step, 1)] = value[None, size_y - EDGE :]
                edge_down[number, pl.ds(step, 1)] = value[None, size_y - 1 :]

    @pl.when(step == 0)
    def _():
        for number, member in enumerate(PLUS_X):
            face_up[number] = out[member, 0]
        for number, member in enumerate(CORNERS):
            row = 0 if VELOCITY_TABLE[member][1] == 1 else size_y - 1
            if VELOCITY_TABLE[member][0] == 1:
                corner_out[number][...] = out[member, 0, row : row + 1]

    @pl.when(step == size_x - 1)
    def _():
        for number, member in enumerate(MINUS_X):
            face_down[number] = out[member, 0]
        for number, member in enumerate(CORNERS):
            row = 0 if VELOCITY_TABLE[member][1] == 1 else size_y - 1
            if VELOCITY_TABLE[member][0] == -1:
                corner_out[number][...] = out[member, 0, row : row + 1]


def patch(old, face_up, face_down, block_up, block_down, edge_up, edge_down, *refs):
    del old
    corners = refs[:4]
    out, plane_up, plane_down, rows_up, rows_down, done = refs[4:]
    size_x, size_y = out.shape[1], out.shape[2]
    copies = []
    for table, source, target, place in (
        (PLUS_X, face_up, plane_up, 0),
        (MINUS_X, face_down, plane_down, size_x - 1),
    ):
        for number, member in enumerate(table):
            target[number] = source[number]
            if member in CORNERS:
                row = 0 if VELOCITY_TABLE[member][1] == 1 else size_y - 1
                target[number, row : row + 1] = corners[CORNERS.index(member)][...]
            copies.append(
                pltpu.make_async_copy(
                    target.at[number], out.at[member, place], done.at[len(copies)]
                )
            )
            copies[-1].start()
    for table, source, line, target, place, row in (
        (PLUS_Y, block_up, edge_up, rows_up, 0, 0),
        (MINUS_Y, block_down, edge_down, rows_down, size_y - EDGE, EDGE - 1),
    ):
        for number, member in enumerate(table):
            target[number] = source[number]
            target[number, :, row : row + 1] = line[number]
            first = 1 if VELOCITY_TABLE[member][0] == 1 else 0
            count = size_x - abs(VELOCITY_TABLE[member][0])
            copies.append(
                pltpu.make_async_copy(
                    target.at[number, pl.ds(first, count)],
                    out.at[member, pl.ds(first, count), pl.ds(place, EDGE)],
                    done.at[len(copies)],
                )
            )
            copies[-1].start()
    for copy in copies:
        copy.wait()


def local(
    populations, rotation_init, slot_cell, slot_count, marker_arm, marker_area, marker_fraction
):
    size_x, size_y, depth = (populations.shape[1], populations.shape[2], populations.shape[3])
    slots = marker_area.shape[2]
    planes = size_x * size_y
    coord_x = slot_cell[0].reshape(1, slots) - lax.axis_index("gx") * size_x
    coord_y = slot_cell[1].reshape(1, slots) - lax.axis_index("gy") * size_y
    coord_z = slot_cell[2].reshape(1, slots)
    plane = coord_x * size_y + coord_y
    after = (coord_z + 1) % depth
    cell = plane * depth + coord_z
    following = plane * depth + after
    zero = jnp.zeros_like(cell)
    ints = jnp.concatenate([cell, following, plane, coord_z, after, zero, zero, zero], axis=0)
    cols = jnp.concatenate([cell.reshape(slots, 1), following.reshape(slots, 1)], axis=1)
    active = lax.broadcasted_iota(jnp.int32, (1, slots), 1) < slot_count.reshape(1, 1)
    weight = jnp.where(active, marker_area.reshape(1, slots), 0.0)
    blank = jnp.zeros_like(weight)
    floats = jnp.concatenate(
        [
            marker_arm.reshape(3, slots),
            weight,
            marker_fraction.reshape(1, slots),
            blank,
            blank,
            blank,
        ],
        axis=0,
    )
    f32 = jnp.float32
    smem = pl.BlockSpec(memory_space=pltpu.SMEM)

    def whole(*shape):
        return pl.BlockSpec(shape, lambda i: (0,) * len(shape))

    def struct(*shape):
        return jax.ShapeDtypeStruct(shape, f32)

    density, velocity, vectors, sums = pl.pallas_call(
        front,
        name="front",
        grid=(size_x,),
        in_specs=[
            smem,
            pl.BlockSpec((Q, 1, size_y, depth), lambda i: (0, i, 0, 0)),
            whole(slots, 2),
            whole(8, slots),
            whole(8, slots),
        ],
        out_specs=[
            whole(size_x, size_y, depth),
            whole(3, size_x, size_y, depth),
            whole(16, slots),
            whole(1, 128),
        ],
        out_shape=[
            struct(size_x, size_y, depth),
            struct(3, size_x, size_y, depth),
            struct(16, slots),
            struct(1, 128),
        ],
        scratch_shapes=[
            pltpu.VMEM((3, slots, slots), jnp.bfloat16),
            pltpu.VMEM((6 * depth, planes), jnp.bfloat16),
            pltpu.VMEM((8, slots), f32),
        ],
        compiler_params=pltpu.CompilerParams(dimension_semantics=("arbitrary",)),
    )(rotation_init, populations, cols, ints, floats)
    sums = global_sum(sums)

    def member_spec(member):
        step_x = VELOCITY_TABLE[member][0]
        return pl.BlockSpec(
            (1, 1, size_y, depth),
            lambda i: (member, lax.rem(i + (size_x - step_x), size_x), 0, 0),
        )

    results = pl.pallas_call(
        back,
        name="back",
        grid=(size_x,),
        in_specs=[
            smem,
            whole(1, 128),
            whole(8, slots),
            whole(8, slots),
            whole(16, slots),
            whole(size_x, size_y, depth),
            whole(3, size_x, size_y, depth),
        ]
        + [member_spec(member) for member in range(Q)],
        out_specs=[
            pl.BlockSpec((Q, 1, size_y, depth), lambda i: (0, i, 0, 0)),
            whole(3, 3),
            whole(5, size_y, depth),
            whole(5, size_y, depth),
            whole(5, size_x, EDGE, depth),
            whole(5, size_x, EDGE, depth),
            whole(5, size_x, 1, depth),
            whole(5, size_x, 1, depth),
        ]
        + [whole(1, depth)] * 4,
        out_shape=[
            struct(Q, size_x, size_y, depth),
            struct(3, 3),
            struct(5, size_y, depth),
            struct(5, size_y, depth),
            struct(5, size_x, EDGE, depth),
            struct(5, size_x, EDGE, depth),
            struct(5, size_x, 1, depth),
            struct(5, size_x, 1, depth),
        ]
        + [struct(1, depth)] * 4,
        scratch_shapes=[pltpu.VMEM((3, planes, depth), f32)],
        compiler_params=pltpu.CompilerParams(dimension_semantics=("arbitrary",)),
    )(rotation_init, sums, ints, floats, vectors, density, velocity, *([populations] * Q))
    out, history, face_up, face_down, block_up, block_down, edge_up, edge_down = results[:8]
    face_up = lax.ppermute(face_up, "gx", ring("gx", 1))
    face_down = lax.ppermute(face_down, "gx", ring("gx", -1))
    edge_up = lax.ppermute(edge_up, "gy", ring("gy", 1))
    edge_down = lax.ppermute(edge_down, "gy", ring("gy", -1))
    corners = [
        lax.ppermute(
            results[8 + number],
            ("gx", "gy"),
            diagonal(VELOCITY_TABLE[member][0], VELOCITY_TABLE[member][1]),
        )
        for number, member in enumerate(CORNERS)
    ]
    anywhere = pl.BlockSpec(memory_space=pl.ANY)
    vmem = pl.BlockSpec(memory_space=pltpu.VMEM)
    out = pl.pallas_call(
        patch,
        name="patch",
        in_specs=[anywhere] + [vmem] * 10,
        out_specs=anywhere,
        out_shape=struct(Q, size_x, size_y, depth),
        input_output_aliases={0: 0},
        scratch_shapes=[
            pltpu.VMEM((5, size_y, depth), f32),
            pltpu.VMEM((5, size_y, depth), f32),
            pltpu.VMEM((5, size_x, EDGE, depth), f32),
            pltpu.VMEM((5, size_x, EDGE, depth), f32),
            pltpu.SemaphoreType.DMA((20,)),
        ],
    )(out, face_up, face_down, block_up, block_down, edge_up, edge_down, *corners)
    return out, history


def solution(mesh):
    return jax.shard_map(
        local,
        mesh=mesh,
        in_specs=(
            P(None, "gx", "gy", None),
            P(),
            P(None, "gx", "gy", None),
            P("gx", "gy"),
            P(None, "gx", "gy", None),
            P("gx", "gy", None),
            P("gx", "gy", None),
        ),
        out_specs=(P(None, "gx", "gy", None), P()),
        check_vma=False,
    )
```

```python
import jax
import jax.numpy as jnp
from jax import lax
from jax.experimental import pallas as pl
from jax.experimental.pallas import tpu as pltpu
from jax.sharding import PartitionSpec as P

Q = 19

VELOCITY_TABLE = (
    (0, 0, 0),
    (1, 0, 0),
    (-1, 0, 0),
    (0, 1, 0),
    (0, -1, 0),
    (0, 0, 1),
    (0, 0, -1),
    (1, 1, 0),
    (-1, -1, 0),
    (1, -1, 0),
    (-1, 1, 0),
    (1, 0, 1),
    (-1, 0, -1),
    (1, 0, -1),
    (-1, 0, 1),
    (0, 1, 1),
    (0, -1, -1),
    (0, 1, -1),
    (0, -1, 1),
)
WEIGHT_TABLE = (1.0 / 3.0,) + (1.0 / 18.0,) * 6 + (1.0 / 36.0,) * 12
RELAX_TIME = 0.8
SPREAD_GAIN = 0.25
SPIN_GAIN = 0.5
PLUS_X = [m for m in range(Q) if VELOCITY_TABLE[m][0] == 1]
MINUS_X = [m for m in range(Q) if VELOCITY_TABLE[m][0] == -1]
PLUS_Y = [m for m in range(Q) if VELOCITY_TABLE[m][1] == 1]
MINUS_Y = [m for m in range(Q) if VELOCITY_TABLE[m][1] == -1]
CORNERS = [m for m in range(Q) if VELOCITY_TABLE[m][0] != 0 and VELOCITY_TABLE[m][1] != 0]
LEVER, WEIGHT, FRACTION = 0, 3, 4
CELL, NEXT, PLANE, LOW, HIGH = 0, 1, 2, 3, 4
EDGE = 8


def ring(axis, steps):
    count = lax.axis_size(axis)
    return [(source, (source + steps) % count) for source in range(count)]


def with_corners(edge, face_up, face_down, table, row):
    size_x = edge.shape[1]
    numbers = lax.broadcasted_iota(jnp.int32, edge.shape, 0)
    places = lax.broadcasted_iota(jnp.int32, edge.shape, 1)
    for number, member in enumerate(table):
        if VELOCITY_TABLE[member][0] == 1:
            line, place = face_up[PLUS_X.index(member), row], 0
        elif VELOCITY_TABLE[member][0] == -1:
            line, place = face_down[MINUS_X.index(member), row], size_x - 1
        else:
            continue
        edge = jnp.where((numbers == number) & (places == place), line[None, None, None], edge)
    return edge


def global_sum(value):
    for axis in ("gy", "gx"):
        count = lax.axis_size(axis)
        if count & (count - 1) == 0:
            bit = 1
            while bit < count:
                value = value + lax.ppermute(value, axis, [(i, i ^ bit) for i in range(count)])
                bit *= 2
        else:
            value = lax.psum(value, axis)
    return value


def cross_rows(first, second):
    return [
        first[1] * second[2] - first[2] * second[1],
        first[2] * second[0] - first[0] * second[2],
        first[0] * second[1] - first[1] * second[0],
    ]


def halves(value):
    high = value.astype(jnp.bfloat16)
    return high, (value - high.astype(jnp.float32)).astype(jnp.bfloat16)


def one_hot(hit):
    return jnp.where(hit, 1.0, 0.0).astype(jnp.bfloat16)


def depth_chunk(depth, ints, floats):
    ids = lax.broadcasted_iota(jnp.int32, (depth, ints.shape[1]), 0)
    fraction = floats[FRACTION : FRACTION + 1]
    low = jnp.where(ids == ints[LOW : LOW + 1], 1.0 - fraction, 0.0)
    return low + jnp.where(ids == ints[HIGH : HIGH + 1], fraction, 0.0)


def front(
    spin, live, pops, cells, arms, area, fractions,
    density_out, velocity_out, vector_out, sums_out, ints, floats,
    mask, turned, gathered, cols,
):
    step = pl.program_id(0)
    size_x, size_y, depth = density_out.shape
    slots = ints.shape[1]
    chunk = slots // size_x

    @pl.when(step == 0)
    def _():
        coord_x = lax.rem(cells[0, 0], size_x)
        coord_y = lax.rem(cells[1, 0], size_y)
        coord_z = cells[2, 0]
        plane = coord_x * size_y + coord_y
        after = jnp.where(coord_z == depth - 1, 0, coord_z + 1)
        cell = plane * depth + coord_z
        following = plane * depth + after
        ints[CELL : CELL + 1] = cell
        ints[NEXT : NEXT + 1] = following
        ints[PLANE : PLANE + 1] = plane
        ints[LOW : LOW + 1] = coord_z
        ints[HIGH : HIGH + 1] = after
        active = lax.broadcasted_iota(jnp.int32, (1, slots), 1) < live[0, 0]
        for axis in range(3):
            floats[LEVER + axis : LEVER + axis + 1] = arms[axis, 0]
        floats[WEIGHT : WEIGHT + 1] = jnp.where(active, area[0], 0.0)
        floats[FRACTION : FRACTION + 1] = fractions[0]
        for number, row in enumerate((cell, following)):
            cols[number] = jnp.broadcast_to(row.astype(jnp.float32), (128, slots)).T
    total = pops[0, 0]
    momentum = [None, None, None]
    for member in range(1, Q):
        value = pops[member, 0]
        total = total + value
        for axis in range(3):
            direction = VELOCITY_TABLE[member][axis]
            if direction == 0:
                continue
            if momentum[axis] is None:
                momentum[axis] = value if direction > 0 else -value
            elif direction > 0:
                momentum[axis] = momentum[axis] + value
            else:
                momentum[axis] = momentum[axis] - value
    density_out[step] = total
    inverse = 1.0 / total
    for axis in range(3):
        velocity_out[axis, step] = momentum[axis] * inverse

    start = pl.multiple_of(step * chunk, 128)
    mine = ints[:, pl.ds(start, chunk)].astype(jnp.float32)

    def mask_rows(index, carry):
        row = pl.multiple_of(index * 128, 128)
        low = cols[0, pl.ds(row, 128), :]
        high = cols[1, pl.ds(row, 128), :]
        for lane in range(0, chunk, 128):
            here = pl.ds(pl.multiple_of(start + lane, 128), 128)
            cell = mine[CELL : CELL + 1, lane : lane + 128]
            following = mine[NEXT : NEXT + 1, lane : lane + 128]
            mask[0, pl.ds(row, 128), here] = one_hot(low == cell)
            mask[1, pl.ds(row, 128), here] = one_hot(high == cell)
            mask[2, pl.ds(row, 128), here] = one_hot(low == following)
        return carry

    lax.fori_loop(0, slots // 128, mask_rows, 0)

    def overlap(value):
        fraction = floats[FRACTION : FRACTION + 1, :]
        low = (1.0 - fraction) * value
        high = fraction * value
        low_a, low_b = [part.astype(jnp.float32) for part in halves(low)]
        high_a, high_b = [part.astype(jnp.float32) for part in halves(high)]
        both = jnp.concatenate([low_a, high_a, low_b, high_b], axis=0).astype(jnp.bfloat16)
        only_high = jnp.concatenate([high_a, high_b], axis=0).astype(jnp.bfloat16)
        only_low = jnp.concatenate([low_a, low_b], axis=0).astype(jnp.bfloat16)

        def body(index, carry):
            at = pl.multiple_of(index * chunk, 128)
            here = pl.ds(at, chunk)
            same = jnp.dot(both, mask[0, :, here], preferred_element_type=jnp.float32)
            up = jnp.dot(only_high, mask[1, :, here], preferred_element_type=jnp.float32)
            down = jnp.dot(only_low, mask[2, :, here], preferred_element_type=jnp.float32)
            at_low = same[0:8] + same[16:24] + up[0:8] + up[8:16]
            at_high = same[8:16] + same[24:32] + down[0:8] + down[8:16]
            part = floats[FRACTION : FRACTION + 1, here]
            gathered[:, here] = (1.0 - part) * at_low + part * at_high
            return carry

        lax.fori_loop(0, size_x, body, 0)
        return gathered[...]

    @pl.when(step == size_x - 1)
    def _():
        planes = size_x * size_y
        for axis in range(3):
            field = velocity_out[axis].reshape(planes, depth).T
            high, low = halves(field)
            turned[2 * axis * depth : (2 * axis + 1) * depth] = high
            turned[(2 * axis + 1) * depth : (2 * axis + 2) * depth] = low

        def sample(index, carry):
            here = pl.ds(pl.multiple_of(index * chunk, 128), chunk)
            ids = lax.broadcasted_iota(jnp.int32, (planes, chunk), 0)
            table = one_hot(ids == ints[PLANE : PLANE + 1, here])
            weights = depth_chunk(depth, ints[:, here], floats[:, here])
            for axis in range(3):
                rows = jnp.dot(
                    turned[2 * axis * depth : (2 * axis + 2) * depth],
                    table,
                    preferred_element_type=jnp.float32,
                )
                rows = rows[:depth] + rows[depth:]
                gathered[axis : axis + 1, here] = jnp.sum(rows * weights, axis=0, keepdims=True)
            return carry

        lax.fori_loop(0, size_x, sample, 0)
        lever = [floats[LEVER + axis : LEVER + axis + 1, :] for axis in range(3)]
        weight = floats[WEIGHT : WEIGHT + 1, :]
        target = cross_rows([spin[0], spin[1], spin[2]], lever)
        error = [target[axis] - gathered[axis : axis + 1, :] for axis in range(3)]
        blank = jnp.zeros_like(weight)
        stacked = jnp.concatenate(error + lever + [blank, blank], axis=0)
        second = stacked - SPREAD_GAIN * overlap(weight * stacked)
        third = second - SPREAD_GAIN * overlap(weight * second)
        second_rows = [second[axis : axis + 1] for axis in range(6)]
        third_rows = [third[axis : axis + 1] for axis in range(3)]
        arm = [weight * row for row in lever]
        products = []
        for rows in (error, second_rows[:3], third_rows):
            products += cross_rows(arm, rows)
        for rows in (lever, second_rows[3:]):
            products += [rows[i] * arm[j] for i in range(3) for j in range(3)]
        products += [blank] * (32 - len(products))
        products = jnp.concatenate(products, axis=0)
        reduced = jnp.sum(products, axis=1, keepdims=True)
        row_ids = lax.broadcasted_iota(jnp.int32, (32, 128), 0)
        lane_ids = lax.broadcasted_iota(jnp.int32, (32, 128), 1)
        picked = jnp.where(row_ids == lane_ids, reduced, 0.0)
        sums_out[...] = jnp.sum(picked, axis=0, keepdims=True)
        static = [weight * (error[i] + second_rows[i] + third_rows[i]) for i in range(3)]
        moved = [weight * row for row in second_rows[3:]]
        vector_out[...] = jnp.concatenate(static + arm + moved + [blank] * 7, axis=0)


def back(
    spin, sums, ints, floats, vectors, density, velocity, pops,
    out, history, face_up, face_down, block_up, block_down, edge_up, edge_down,
    field, members, arrived,
):
    step = pl.program_id(0)
    size_x, size_y, depth = density.shape
    planes = size_x * size_y
    slots = ints.shape[1]
    chunk = slots // size_x
    copies = [
        pltpu.make_async_copy(pops.at[:, place], members.at[:, place], arrived.at[place])
        for place in range(size_x)
    ]

    @pl.when(step == 0)
    def _():
        for copy in copies:
            copy.start()
        entry = [sums[0:1, i : i + 1] for i in range(27)]
        direct, moved = entry[9:18], entry[18:27]
        inertia = direct[0] + direct[4] + direct[8]
        trace = moved[0] + moved[4] + moved[8]

        def turn(table, diagonal_sum, delta):
            return [
                diagonal_sum * delta[i]
                - (table[3 * i] * delta[0] + table[3 * i + 1] * delta[1] + table[3 * i + 2] * delta[2])
                for i in range(3)
            ]

        scale = -SPIN_GAIN / inertia
        first = [scale * value for value in entry[0:3]]
        extra = turn(direct, inertia, first)
        second = [scale * (entry[3 + i] + extra[i]) for i in range(3)]
        late = turn(moved, trace, first)
        extra = turn(direct, inertia, second)
        third = [scale * (entry[6 + i] + late[i] + extra[i]) for i in range(3)]
        row_ids = lax.broadcasted_iota(jnp.int32, (3, 3), 0)
        lane_ids = lax.broadcasted_iota(jnp.int32, (3, 3), 1)
        result = jnp.zeros((3, 3), jnp.float32)
        for axis in range(3):
            one = spin[axis] + first[axis]
            two = one + second[axis]
            three = two + third[axis]
            value = jnp.where(row_ids == 0, one, jnp.where(row_ids == 1, two, three))
            result = jnp.where(lane_ids == axis, value, result)
        history[...] = result
        both = [first[i] + second[i] for i in range(3)]
        for axis in range(3):
            field[axis] = velocity[axis].reshape(planes, depth)

        def spread(index, carry):
            here = pl.ds(pl.multiple_of(index * chunk, 128), chunk)
            lever = [vectors[3 + i : 4 + i, here] for i in range(3)]
            bent = [vectors[6 + i : 7 + i, here] for i in range(3)]
            plain = cross_rows(both, lever)
            after = cross_rows(first, bent)
            ids = lax.broadcasted_iota(jnp.int32, (planes, chunk), 0)
            table = one_hot(ids == ints[PLANE : PLANE + 1, here])
            weights = depth_chunk(depth, ints[:, here], floats[:, here])
            for axis in range(3):
                impulse = SPREAD_GAIN * (vectors[axis : axis + 1, here] + plain[axis] + after[axis])
                high, low = halves(weights * impulse)
                added = lax.dot_general(
                    table, high, (((1,), (1,)), ((), ())), preferred_element_type=jnp.float32
                )
                added = added + lax.dot_general(
                    table, low, (((1,), (1,)), ((), ())), preferred_element_type=jnp.float32
                )
                field[axis] = field[axis] + added
            return carry

        lax.fori_loop(0, size_x, spread, 0)
        for copy in copies:
            copy.wait()

    def fields_at(place):
        place_rows = pl.ds(pl.multiple_of(place * size_y, 8), size_y)
        u = [field[axis, place_rows, :] for axis in range(3)]
        base = 1.0 - 1.5 * (u[0] * u[0] + u[1] * u[1] + u[2] * u[2])
        return u, base, density[place] * (1.0 / RELAX_TIME)

    for step_x in (0, 1, -1):
        place = lax.rem(step + (size_x - step_x), size_x)
        u, base, scaled = fields_at(place)
        for member in range(Q):
            velocity_here = VELOCITY_TABLE[member]
            if velocity_here[0] != step_x:
                continue
            projected = None
            for axis in range(3):
                if velocity_here[axis] == 0:
                    continue
                term = u[axis] if velocity_here[axis] > 0 else -u[axis]
                projected = term if projected is None else projected + term
            shape = base
            if projected is not None:
                shape = base + projected * (3.0 + 4.5 * projected)
            value = (1.0 - 1.0 / RELAX_TIME) * members[member, place] + (
                WEIGHT_TABLE[member] * scaled
            ) * shape
            if velocity_here[1] != 0:
                value = pltpu.roll(value, velocity_here[1] % size_y, 0)
            if velocity_here[2] != 0:
                value = pltpu.roll(value, velocity_here[2] % depth, 1)
            out[member, 0] = value
            if velocity_here[1] == 1:
                number = PLUS_Y.index(member)
                block_up[number, pl.ds(step, 1)] = value[None, :EDGE]
                edge_up[number, pl.ds(step, 1)] = value[None, 0:1]
            if velocity_here[1] == -1:
                number = MINUS_Y.index(member)
                block_down[number, pl.ds(step, 1)] = value[None, size_y - EDGE :]
                edge_down[number, pl.ds(step, 1)] = value[None, size_y - 1 :]

    @pl.when(step == 0)
    def _():
        for number, member in enumerate(PLUS_X):
            face_up[number] = out[member, 0]

    @pl.when(step == size_x - 1)
    def _():
        for number, member in enumerate(MINUS_X):
            face_down[number] = out[member, 0]


def patch(
    old, face_up, face_down, block_up, block_down, edge_up, edge_down,
    out, plane_up, plane_down, rows_up, rows_down, done,
):
    del old
    size_x, size_y = out.shape[1], out.shape[2]
    copies = []
    for table, source, target, place in (
        (PLUS_X, face_up, plane_up, 0),
        (MINUS_X, face_down, plane_down, size_x - 1),
    ):
        for number, member in enumerate(table):
            target[number] = source[number]
            if member in CORNERS:
                if VELOCITY_TABLE[member][1] == 1:
                    target[number, 0:1] = edge_up[PLUS_Y.index(member), place]
                else:
                    target[number, size_y - 1 :] = edge_down[MINUS_Y.index(member), place]
            copies.append(
                pltpu.make_async_copy(
                    target.at[number], out.at[member, place], done.at[len(copies)]
                )
            )
            copies[-1].start()
    for table, source, line, target, place, row in (
        (PLUS_Y, block_up, edge_up, rows_up, 0, 0),
        (MINUS_Y, block_down, edge_down, rows_down, size_y - EDGE, EDGE - 1),
    ):
        for number, member in enumerate(table):
            target[number] = source[number]
            target[number, :, row : row + 1] = line[number]
            first = 1 if VELOCITY_TABLE[member][0] == 1 else 0
            count = size_x - abs(VELOCITY_TABLE[member][0])
            copies.append(
                pltpu.make_async_copy(
                    target.at[number, pl.ds(first, count)],
                    out.at[member, pl.ds(first, count), pl.ds(place, EDGE)],
                    done.at[len(copies)],
                )
            )
            copies[-1].start()
    for copy in copies:
        copy.wait()


def local(
    populations, rotation_init, slot_cell, slot_count, marker_arm, marker_area, marker_fraction
):
    size_x, size_y, depth = (populations.shape[1], populations.shape[2], populations.shape[3])
    slots = marker_area.shape[2]
    planes = size_x * size_y
    f32 = jnp.float32
    smem = pl.BlockSpec(memory_space=pltpu.SMEM)

    def whole(*shape):
        return pl.BlockSpec(shape, lambda i: (0,) * len(shape))

    def struct(*shape):
        return jax.ShapeDtypeStruct(shape, f32)

    density, velocity, vectors, sums, ints, floats = pl.pallas_call(
        front,
        name="front",
        grid=(size_x,),
        in_specs=[
            smem,
            smem,
            pl.BlockSpec((Q, 1, size_y, depth), lambda i: (0, i, 0, 0)),
            whole(3, 1, 1, slots),
            whole(3, 1, 1, slots),
            whole(1, 1, slots),
            whole(1, 1, slots),
        ],
        out_specs=[
            whole(size_x, size_y, depth),
            whole(3, size_x, size_y, depth),
            whole(16, slots),
            whole(1, 128),
            whole(8, slots),
            whole(8, slots),
        ],
        out_shape=[
            struct(size_x, size_y, depth),
            struct(3, size_x, size_y, depth),
            struct(16, slots),
            struct(1, 128),
            jax.ShapeDtypeStruct((8, slots), jnp.int32),
            struct(8, slots),
        ],
        scratch_shapes=[
            pltpu.VMEM((3, slots, slots), jnp.bfloat16),
            pltpu.VMEM((6 * depth, planes), jnp.bfloat16),
            pltpu.VMEM((8, slots), f32),
            pltpu.VMEM((2, slots, 128), f32),
        ],
        compiler_params=pltpu.CompilerParams(dimension_semantics=("arbitrary",)),
    )(rotation_init, slot_count, populations, slot_cell, marker_arm, marker_area, marker_fraction)
    sums = global_sum(sums)

    results = pl.pallas_call(
        back,
        name="back",
        grid=(size_x,),
        in_specs=[
            smem,
            whole(1, 128),
            whole(8, slots),
            whole(8, slots),
            whole(16, slots),
            whole(size_x, size_y, depth),
            whole(3, size_x, size_y, depth),
            pl.BlockSpec(memory_space=pl.ANY),
        ],
        out_specs=[
            pl.BlockSpec((Q, 1, size_y, depth), lambda i: (0, i, 0, 0)),
            whole(3, 3),
            whole(5, size_y, depth),
            whole(5, size_y, depth),
            whole(5, size_x, EDGE, depth),
            whole(5, size_x, EDGE, depth),
            whole(5, size_x, 1, depth),
            whole(5, size_x, 1, depth),
        ],
        out_shape=[
            struct(Q, size_x, size_y, depth),
            struct(3, 3),
            struct(5, size_y, depth),
            struct(5, size_y, depth),
            struct(5, size_x, EDGE, depth),
            struct(5, size_x, EDGE, depth),
            struct(5, size_x, 1, depth),
            struct(5, size_x, 1, depth),
        ],
        scratch_shapes=[
            pltpu.VMEM((3, planes, depth), f32),
            pltpu.VMEM((Q, size_x, size_y, depth), f32),
            pltpu.SemaphoreType.DMA((size_x,)),
        ],
        compiler_params=pltpu.CompilerParams(dimension_semantics=("arbitrary",)),
    )(rotation_init, sums, ints, floats, vectors, density, velocity, populations)
    out, history, face_up, face_down, block_up, block_down, edge_up, edge_down = results
    face_up = lax.ppermute(face_up, "gx", ring("gx", 1))
    face_down = lax.ppermute(face_down, "gx", ring("gx", -1))
    edge_up = lax.ppermute(
        with_corners(edge_up, face_up, face_down, PLUS_Y, 0), "gy", ring("gy", 1)
    )
    edge_down = lax.ppermute(
        with_corners(edge_down, face_up, face_down, MINUS_Y, size_y - 1), "gy", ring("gy", -1)
    )
    anywhere = pl.BlockSpec(memory_space=pl.ANY)
    vmem = pl.BlockSpec(memory_space=pltpu.VMEM)
    out = pl.pallas_call(
        patch,
        name="patch",
        in_specs=[anywhere] + [vmem] * 6,
        out_specs=anywhere,
        out_shape=struct(Q, size_x, size_y, depth),
        input_output_aliases={0: 0},
        scratch_shapes=[
            pltpu.VMEM((5, size_y, depth), f32),
            pltpu.VMEM((5, size_y, depth), f32),
            pltpu.VMEM((5, size_x, EDGE, depth), f32),
            pltpu.VMEM((5, size_x, EDGE, depth), f32),
            pltpu.SemaphoreType.DMA((20,)),
        ],
    )(out, face_up, face_down, block_up, block_down, edge_up, edge_down)
    return out, history


def solution(mesh):
    return jax.shard_map(
        local,
        mesh=mesh,
        in_specs=(
            P(None, "gx", "gy", None),
            P(),
            P(None, "gx", "gy", None),
            P("gx", "gy"),
            P(None, "gx", "gy", None),
            P("gx", "gy", None),
            P("gx", "gy", None),
        ),
        out_specs=(P(None, "gx", "gy", None), P()),
        check_vma=False,
    )
```
